32 devices in a mesh: gx: 4 (over z), gy: 8 (over y, x, core).
Axes of the slice: x: 2, y: 2, z: 4, core: 2. Of those that a mesh axis runs over, the one named last changes fastest.
Arguments:
- initial_field: float32 [8, 32, 2048], P(None, 'gx', 'gy'), may hold values from -6 to 6
- target_field: float32 [8, 32, 2048], P(None, 'gx', 'gy'), may hold values from -8 to 8
- land_mask: int32 [32, 2048], P('gx', 'gy'), may hold values 0 or 1
- conv_one: float32 [64, 73], replicated, may hold values from -0.75 to 0.75
- conv_two: float32 [64, 577], replicated, may hold values from -0.25 to 0.25
- head_weights: float32 [32, 65], replicated, may hold values from -0.75 to 0.75
- dir_one: float32 [64, 73], replicated, may hold values from -6 to 6
- dir_two: float32 [64, 577], replicated, may hold values from -6 to 6
- dir_three: float32 [32, 65], replicated, may hold values from -6 to 6
- group_ids: int32 [160], replicated, may hold values from 0 to 5, as said below
Outputs:
- final_field: float32 [8, 32, 2048], P(None, 'gx', 'gy')
- update_one: float32 [64, 73], replicated
- update_two: float32 [64, 577], replicated
- update_three: float32 [32, 65], replicated
The draws below stay inside these ranges and needn't reach their ends.
Inputs may be any that keep to these rules, and one draw needn't show every extreme that they name: `group_ids`: each of the 6 group numbers names 26 or 27 rows.
All inputs are finite; a program needn't handle non-finite values. No bound on the sum of `land_mask` on one device may be relied on, other than what follows from the above.
Results may differ from the reference program's by a relative error of at most 0.0024.
The reference program's roundings to bfloat16 on the way count: a program that leaves them out, or rounds other values in their place, can miss the bound.
Values may be sent and summed in bfloat16 or wider, within the bound.
A program may use at most 64 MiB of HBM per device.

```python
import math
import jax
import jax.numpy as jnp
from jax import lax

LEV = 8
C = 64
K = 32
STEPS = 2
GROUPS = 6
NX = 32
NY = 2048
ROWS = 160
PARAMS = 43680


def draw_target_field(key, part):
    sample = jax.random.normal(key, (LEV, NX, NY), jnp.float32)
    position = jnp.arange(NX, dtype=jnp.float32)[None, :, None] / NX
    values = sample * 3.0 ** position
    return jnp.clip(values, -8.0, 8.0)


def draw_group_ids(key, part):
    return (jax.random.permutation(key, ROWS) % GROUPS).astype(jnp.int32)


def touch_ends(result, rng, low, largest):
    longest = result.shape.index(max(result.shape))
    spots = []
    for shift in (0, 1):
        where = [jax.random.randint(jax.random.fold_in(rng, axis), (), 0, length) for axis, length in enumerate(result.shape)]
        where[longest] = (where[longest] + shift) % result.shape[longest]
        spots.append(tuple(where))
    return result.at[spots[0]].set(low).at[spots[1]].set(largest)


def steps_of(key, shape, cuts, least, largest):
    gain, own = 1.0, jax.random.fold_in(key, 6)
    for dim, shards_of in cuts:
        steps = jnp.exp(jax.random.uniform(jax.random.fold_in(own, dim), (shards_of,), jnp.float32, least / len(cuts), largest / len(cuts)))
        gain = gain * jnp.repeat(steps, shape[dim] // shards_of).reshape([-1 if axis == dim else 1 for axis in range(len(shape))])
    return gain


def gaussian(key, extent, scale, limit, split=(), kind=jnp.bfloat16):
    entries = scale * jax.random.normal(key, extent, jnp.float32)
    if split:
        entries = entries * steps_of(key, extent, split, -0.22, 0.18)
    return jnp.clip(entries, -limit, limit).astype(kind)


def setup_inputs(seed: int = 0) -> dict:
    arg_keys = jax.random.split(jax.random.key(seed), 11)
    return {
        "initial_field": gaussian(arg_keys[0], (LEV, NX, NY), 1.0, 6.0, ((1, 4), (2, 8)), jnp.float32),
        "target_field": draw_target_field(jax.random.fold_in(arg_keys[10], 71), 0),
        "land_mask": touch_ends((jax.random.randint(arg_keys[2], (NX, NY), 0, 4) < 3).astype(jnp.int32), jax.random.fold_in(arg_keys[2], 1), 0, 1),
        "conv_one": gaussian(arg_keys[3], (C, 9 * LEV + 1), (9 * LEV) ** -0.5, 0.75, (), jnp.float32),
        "conv_two": gaussian(arg_keys[4], (C, 9 * C + 1), (9 * C) ** -0.5, 0.25, (), jnp.float32),
        "head_weights": gaussian(arg_keys[5], (K, C + 1), C ** -0.5, 0.75, (), jnp.float32),
        "dir_one": gaussian(arg_keys[6], (C, 9 * LEV + 1), 1.0, 6.0, (), jnp.float32),
        "dir_two": gaussian(arg_keys[7], (C, 9 * C + 1), 1.0, 6.0, (), jnp.float32),
        "dir_three": gaussian(arg_keys[8], (K, C + 1), 1.0, 6.0, (), jnp.float32),
        "group_ids": draw_group_ids(jax.random.fold_in(arg_keys[10], 71), 0),
    }


OFFSETS = ((0, 0), (0, 1), (0, 2), (1, 0), (1, 1), (1, 2), (2, 0), (2, 1), (2, 2))
CONTRACT_ROWS = (((1,), (1,)), ((), ()))
CONTRACT_COLS = (((0,), (0,)), ((), ()))

def silu_parts(activation):
    logistic = jax.nn.sigmoid(activation)
    return (activation * logistic, logistic * (1.0 + activation * (1.0 - logistic)))

def convolve(padded, kernel, bias_column):
    inputs = padded.shape[0]
    height = padded.shape[1] - 2
    breadth = padded.shape[2] - 2
    summed = jnp.zeros((kernel.shape[0], height * breadth), jnp.float32)
    for offset_index, offset_pair in enumerate(OFFSETS):
        row_start, col_start = offset_pair
        window = padded[:, row_start:row_start + height, col_start:col_start + breadth].reshape(inputs, height * breadth)
        weight_block = kernel[:, offset_index * inputs:(offset_index + 1) * inputs]
        summed = summed + jnp.dot(weight_block, window, preferred_element_type=jnp.float32)
    return summed.reshape(-1, height, breadth) + bias_column[:, None, None]

def convolve_back(padded, kernel, errors, precision):
    inputs = padded.shape[0]
    height = padded.shape[1] - 2
    breadth = padded.shape[2] - 2
    flat_error = errors.reshape(errors.shape[0], height * breadth)
    pieces = []
    input_grad = jnp.zeros(padded.shape, jnp.float32)
    for offset_index, offset_pair in enumerate(OFFSETS):
        row_start, col_start = offset_pair
        window = padded[:, row_start:row_start + height, col_start:col_start + breadth].reshape(inputs, height * breadth)
        pieces.append(lax.dot_general(flat_error, window, CONTRACT_ROWS, precision=precision, preferred_element_type=jnp.float32))
        weight_block = kernel[:, offset_index * inputs:(offset_index + 1) * inputs]
        carried = lax.dot_general(weight_block, flat_error, CONTRACT_COLS, precision=precision, preferred_element_type=jnp.float32)
        input_grad = input_grad.at[:, row_start:row_start + height, col_start:col_start + breadth].add(carried.reshape(inputs, height, breadth))
    return (jnp.concatenate(pieces, axis=1), input_grad)

def neighbours(padded):
    return (padded[:, 2:, 1:-1], padded[:, :-2, 1:-1], padded[:, 1:-1, 2:], padded[:, 1:-1, :-2])

def advance(padded, coeffs, wet_cells):
    center = padded[:, 1:-1, 1:-1]
    change = jnp.zeros(center.shape, jnp.float32)
    for direction, beside in enumerate(neighbours(padded)):
        change = change + coeffs[direction] * (beside - center)
    return center + wet_cells * change

def advance_back(padded, coeffs, wet_cells, adjoint):
    center = padded[:, 1:-1, 1:-1]
    weighted = wet_cells * adjoint
    grad_coeffs = []
    remains = adjoint
    for direction, beside in enumerate(neighbours(padded)):
        grad_coeffs.append(weighted * (beside - center))
        remains = remains - weighted * coeffs[direction]
    carried = weighted * coeffs
    grad_pad = jnp.zeros(padded.shape, jnp.float32)
    grad_pad = grad_pad.at[:, 2:, 1:-1].add(carried[0])
    grad_pad = grad_pad.at[:, :-2, 1:-1].add(carried[1])
    grad_pad = grad_pad.at[:, 1:-1, 2:].add(carried[2])
    grad_pad = grad_pad.at[:, 1:-1, :-2].add(carried[3])
    grad_pad = grad_pad.at[:, 1:-1, 1:-1].add(remains)
    return (jnp.stack(grad_coeffs), grad_pad)

def split_kernels(conv_one, conv_two, head_weights):
    return [(weights[:, :-1].astype(jnp.bfloat16), weights[:, -1]) for weights in (conv_one, conv_two, head_weights)]

def tail_forward(hidden_pad, kernels):
    second_pre = convolve(hidden_pad, kernels[1][0], kernels[1][1])
    second_out = silu_parts(second_pre)[0].astype(jnp.bfloat16)
    channels = second_out.shape[0]
    height = second_out.shape[1]
    breadth = second_out.shape[2]
    head_pre = jnp.dot(kernels[2][0], second_out.reshape(channels, height * breadth), preferred_element_type=jnp.float32) + kernels[2][1][:, None]
    logistic = jax.nn.sigmoid(head_pre)
    coeffs = (0.25 * logistic).reshape(4, -1, height, breadth)
    return (second_pre, second_out, logistic, coeffs)

def tail_back(hidden_pad, kernels, stored_tail, grad_coeffs):
    second_pre, second_out, logistic, coeffs = stored_tail
    head_error = grad_coeffs.reshape(logistic.shape) * (0.25 * logistic * (1.0 - logistic))
    head_round = head_error.astype(jnp.bfloat16)
    flat_out = second_out.reshape(second_out.shape[0], -1)
    head_grad = jnp.concatenate([lax.dot_general(head_round, flat_out, CONTRACT_ROWS, preferred_element_type=jnp.float32), lax.optimization_barrier(jnp.sum(head_error, axis=1))[:, None]], axis=1)
    hidden_back = lax.dot_general(kernels[2][0], head_round, CONTRACT_COLS, preferred_element_type=jnp.float32)
    second_error = hidden_back.reshape(second_pre.shape) * silu_parts(second_pre)[1]
    weight_grad, hidden_grad = convolve_back(hidden_pad, kernels[1][0], second_error.astype(jnp.bfloat16), None)
    second_grad = jnp.concatenate([weight_grad, lax.optimization_barrier(jnp.sum(second_error, axis=(1, 2)))[:, None]], axis=1)
    return (head_grad, second_grad, hidden_grad)

def first_back(tracer_round, kernel, first_error):
    first_round = first_error.astype(jnp.bfloat16)
    weight_grad, tracer_grad = convolve_back(tracer_round, kernel, first_round, None)
    return (jnp.concatenate([weight_grad, lax.optimization_barrier(jnp.sum(first_error, axis=(1, 2)))[:, None]], axis=1), tracer_grad)

def finish(gradients, directions, group_ids):
    norm_total = jnp.zeros((), jnp.float32)
    for member in gradients:
        norm_total = norm_total + jnp.sum(member * member)
    factor = 1.0 / jnp.maximum(jnp.sqrt(norm_total), 1.0)
    clipped = [member * factor for member in gradients]
    clip_rows = jnp.concatenate([lax.optimization_barrier(jnp.sum(member * member, axis=1)) for member in clipped])
    dir_rows = jnp.concatenate([lax.optimization_barrier(jnp.sum(member * member, axis=1)) for member in directions])
    choose = (group_ids[:, None] == jnp.arange(GROUPS, dtype=jnp.int32)[None, :]).astype(jnp.float32)
    ratios = jnp.sqrt(lax.optimization_barrier(jnp.sum(choose * clip_rows[:, None], axis=0))) / jnp.sqrt(lax.optimization_barrier(jnp.sum(choose * dir_rows[:, None], axis=0)) + 1e-06)
    row_ratio = lax.optimization_barrier(jnp.sum(choose * ratios[None, :], axis=1))
    scaling = math.sqrt(PARAMS)
    outputs = []
    row_start = 0
    for member, heading in zip(clipped, directions):
        row_count = member.shape[0]
        outputs.append(scaling * (member + row_ratio[row_start:row_start + row_count, None] * heading))
        row_start = row_start + row_count
    return outputs

def step_forward(tracer, kernels, wet_cells):
    tracer_pad = jnp.pad(tracer, ((0, 0), (1, 1), (1, 1)))
    tracer_round = tracer_pad.astype(jnp.bfloat16)
    first_pre = convolve(tracer_round, kernels[0][0], kernels[0][1])
    hidden = silu_parts(first_pre)[0].astype(jnp.bfloat16)
    hidden_pad = jnp.pad(hidden, ((0, 0), (1, 1), (1, 1)))
    stored_tail = tail_forward(hidden_pad, kernels)
    return (advance(tracer_pad, stored_tail[3], wet_cells), (tracer_pad, tracer_round, first_pre, hidden_pad, stored_tail))

def reference(initial_field, target_field, land_mask, conv_one, conv_two, head_weights, dir_one, dir_two, dir_three, group_ids):
    wet_cells = land_mask.astype(jnp.float32)
    kernels = split_kernels(conv_one, conv_two, head_weights)
    tracer = wet_cells * initial_field
    history = [tracer]
    for step_index in range(STEPS):
        tracer = step_forward(tracer, kernels, wet_cells)[0]
        history.append(tracer)
    final_field = tracer
    adjoint = wet_cells * (tracer - target_field)
    totals = [jnp.zeros(conv_one.shape, jnp.float32), jnp.zeros(conv_two.shape, jnp.float32), jnp.zeros(head_weights.shape, jnp.float32)]
    for step_index in reversed(range(STEPS)):
        stored = step_forward(history[step_index], kernels, wet_cells)[1]
        tracer_pad, tracer_round, first_pre, hidden_pad, stored_tail = stored
        grad_coeffs, near_grad = advance_back(tracer_pad, stored_tail[3], wet_cells, adjoint)
        head_grad, second_grad, hidden_grad = tail_back(hidden_pad, kernels, stored_tail, grad_coeffs)
        first_error = hidden_grad[:, 1:-1, 1:-1] * silu_parts(first_pre)[1]
        first_grad, conv_grad = first_back(tracer_round, kernels[0][0], first_error)
        adjoint = (conv_grad + near_grad)[:, 1:-1, 1:-1]
        totals = [totals[0] + first_grad, totals[1] + second_grad, totals[2] + head_grad]
    updates = finish(totals, [dir_one, dir_two, dir_three], group_ids)
    return (final_field, updates[0], updates[1], updates[2])
```

```python
import functools
import math

import jax
import jax.numpy as jnp
from jax import lax
from jax.experimental import pallas as pl
from jax.experimental.pallas import tpu as pltpu
from jax.sharding import PartitionSpec as P

GROUPS = 6
PARAMS = 43680
RIM = 6
LEV = 8
C = 64
K = 32
TILE = 128
MESH = pl.DeviceIdType.MESH
F32 = jnp.float32
BF16 = jnp.bfloat16
VM = pl.BlockSpec(memory_space=pltpu.VMEM)
LIMIT = 56 * 1024 * 1024
NT = (((1,), (1,)), ((), ()))


def dot(a, b):
    return jnp.dot(a, b, preferred_element_type=F32)


def dot_nt(a, b):
    return lax.dot_general(a, b, NT, preferred_element_type=F32)


def sigmoid(v):
    return 0.5 * jnp.tanh(0.5 * v) + 0.5


def halo_kernel(sizes, field, target, mask, own, left, right, send_sem, recv_sem):
    n_gx, n_gy = sizes
    gx = lax.axis_index("gx")
    gy = lax.axis_index("gy")
    h, width = mask.shape
    for r in range(h):
        wet = jnp.broadcast_to(mask[r : r + 1, :].astype(F32), (LEV, width))
        own[RIM + r, 0:8, :] = wet * field[:, r, :]
        own[RIM + r, 8:16, :] = wet
        own[RIM + r, 16:24, :] = target[:, r, :]

    middle = pl.ds(RIM, h)
    top = pl.ds(0, RIM)
    bottom = pl.ds(RIM + h, RIM)
    first = pl.ds(RIM, RIM)
    last = pl.ds(h, RIM)
    all_lanes = pl.ds(0, width)
    low = pl.ds(0, TILE)
    high = pl.ds(width - TILE, TILE)
    rows_of = {1: (last, top), 0: (middle, middle), -1: (first, bottom)}
    lanes_of = {1: (high, left, low), 0: (all_lanes, own, all_lanes), -1: (low, right, low)}
    moves = [(dx, dy) for dx in (-1, 0, 1) for dy in (-1, 0, 1) if (dx, dy) != (0, 0)]

    def exists(dx, dy):
        x = gx + dx
        y = gy + dy
        return (x >= 0) & (x < n_gx) & (y >= 0) & (y < n_gy)

    barrier = pltpu.get_barrier_semaphore()
    count = jnp.int32(0)
    for dx, dy in moves:
        @pl.when(exists(dx, dy))
        def _():
            pl.semaphore_signal(barrier, inc=1, device_id=(gx + dx, gy + dy), device_id_type=MESH)
        count = count + jnp.where(exists(dx, dy), 1, 0)
    for dx, dy in moves:
        @pl.when(jnp.logical_not(exists(-dx, -dy)))
        def _():
            _, dst_rows = rows_of[dx]
            _, dst, dst_lanes = lanes_of[dy]
            dst[dst_rows, :, dst_lanes] = jnp.zeros((dst_rows.size, 24, dst_lanes.size), F32)
    pl.semaphore_wait(barrier, count)

    copies = []
    for index, (dx, dy) in enumerate(moves):
        src_rows, dst_rows = rows_of[dx]
        src_lanes, dst, dst_lanes = lanes_of[dy]
        copies.append(
            pltpu.make_async_remote_copy(
                src_ref=own.at[src_rows, :, src_lanes],
                dst_ref=dst.at[dst_rows, :, dst_lanes],
                send_sem=send_sem.at[index],
                recv_sem=recv_sem.at[index],
                device_id=(gx + dx, gy + dy),
                device_id_type=MESH,
            )
        )
    for (dx, dy), copy in zip(moves, copies):
        @pl.when(exists(dx, dy))
        def _():
            copy.start()
    for (dx, dy), copy in zip(moves, copies):
        @pl.when(exists(-dx, -dy))
        def _():
            copy.wait_recv()
    for (dx, dy), copy in zip(moves, copies):
        @pl.when(exists(dx, dy))
        def _():
            copy.wait_send()


def roll(v, shift):
    return pltpu.roll(v, shift % v.shape[1], 1)


def compute_kernel(
    sizes, own, left, right, w1_ref, w2_ref, w3_ref,
    final_ref, grads_ref,
    fld, wet_s, tgt, adj, x9, z1, h1, z2, h2, prob, e2m, up, e1m, vv, e3m,
):
    n_gx, n_gy = sizes
    gx = lax.axis_index("gx")
    gy = lax.axis_index("gy")
    rows, _, width = own.shape
    h = rows - 2 * RIM
    wide = width + TILE

    lane = lax.broadcasted_iota(jnp.int32, (LEV, TILE), 1)
    is_right = lane < TILE // 2

    def merge(r, _):
        rest = jnp.where(is_right, right[r, 0:8, :], left[r, 0:8, :])
        fld[0, r] = jnp.concatenate([own[r, 0:8, :], rest], axis=1)
        rest = jnp.where(is_right, right[r, 8:16, :], left[r, 8:16, :])
        wet_s[r] = jnp.concatenate([own[r, 8:16, :], rest], axis=1)
        rest = jnp.where(is_right, right[r, 16:24, :], left[r, 16:24, :])
        tgt[r] = jnp.concatenate([own[r, 16:24, :], rest], axis=1)
        return 0

    lax.fori_loop(0, rows, merge, 0)

    wa = w1_ref[...]
    w1 = wa[:, : 9 * LEV].astype(BF16)
    b1 = wa[:, 9 * LEV :]
    wb = w2_ref[...]
    tap = lambda a, b: wb[:, (3 * a + b) * C : (3 * a + b + 1) * C]
    w2f = jnp.concatenate(
        [jnp.concatenate([tap(a, b) for a in range(3)], axis=1) for b in range(3)], axis=0
    )
    w2 = w2f.astype(BF16)
    w2t = w2f.T.astype(BF16)
    b2 = wb[:, 9 * C :]
    wc = w3_ref[...]
    w3 = wc[:, :C].astype(BF16)
    w3t = wc[:, :C].T.astype(BF16)
    b3 = wc[:, C:]
    w1t = wa[:, : 9 * LEV].T.astype(BF16)

    col_left = jnp.where(gy > 0, 1.0, 0.0).astype(F32)
    col_right = jnp.where(gy < n_gy - 1, 1.0, 0.0).astype(F32)
    side = jnp.where(is_right[0:1], col_right, col_left)
    col_ok = jnp.concatenate([jnp.ones((1, width), F32), side], axis=1)

    def inside(r):
        i = gx * h + r - RIM
        ok = (i >= 0) & (i < n_gx * h)
        return col_ok * jnp.where(ok, 1.0, 0.0).astype(F32)

    def loop(start, stop, body, unroll):
        lax.fori_loop(start, stop, lambda r, c: (body(r), c)[1], 0, unroll=unroll)

    def forward(s, rad):
        def first(r):
            parts = []
            for a in range(3):
                row = fld[s, r + a - 1]
                parts += [roll(row, 1), row, roll(row, -1)]
            cols = jnp.concatenate(parts, axis=0).astype(BF16)
            x9[s, r] = cols
            z = dot(w1, cols) + b1
            z1[s, r] = z
            h1[s, r] = (z * sigmoid(z) * inside(r)).astype(BF16)

        loop(RIM - rad - 1, RIM + h + rad + 1, first, 2)

        def second(r):
            h3 = jnp.concatenate([h1[s, r - 1], h1[s, r], h1[s, r + 1]], axis=0)
            y = dot(w2, h3)
            z = roll(y[0:C], 1) + y[C : 2 * C] + roll(y[2 * C :], -1) + b2
            z2[s, r] = z
            hb = (z * sigmoid(z)).astype(BF16)
            h2[s, r] = hb
            p = sigmoid(dot(w3, hb) + b3)
            prob[s, r] = p
            center = fld[s, r]
            c = 0.25 * p
            change = (
                c[0:8] * (fld[s, r + 1] - center)
                + c[8:16] * (fld[s, r - 1] - center)
                + c[16:24] * (roll(center, -1) - center)
                + c[24:32] * (roll(center, 1) - center)
            )
            fld[s + 1, r] = center + wet_s[r] * change

        loop(RIM - rad, RIM + h + rad, second, 2)

    forward(0, 4)
    forward(1, 2)
    for r in range(h):
        final_ref[:, r, :] = fld[2, RIM + r][:, :width]

    def adjoint_start(r):
        adj[1, r] = wet_s[r] * (fld[2, r] - tgt[r])

    loop(RIM - 2, RIM + h + 2, adjoint_start, 1)

    lane_w = lax.broadcasted_iota(jnp.int32, (1, wide), 1)
    own_lane = jnp.where(lane_w < width, 1.0, 0.0).astype(F32)
    fold = lambda v: sum(v[:, k * TILE : (k + 1) * TILE] for k in range(v.shape[1] // TILE))

    def errors(s, r):
        center = fld[s, r]
        wg = wet_s[r] * adj[s, r]
        p = prob[s, r]
        diff = jnp.concatenate(
            [
                wg * (fld[s, r + 1] - center),
                wg * (fld[s, r - 1] - center),
                wg * (roll(center, -1) - center),
                wg * (roll(center, 1) - center),
            ],
            axis=0,
        )
        e3 = diff * (0.25 * p * (1.0 - p))
        e3b = e3.astype(BF16)
        z = z2[s, r]
        g = sigmoid(z)
        e2 = dot(w3t, e3b) * (g * (1.0 + z * (1.0 - g)))
        return e3, e3b, e2

    def spread(e2):
        return jnp.concatenate([roll(e2, -1), e2, roll(e2, 1)], axis=0).astype(BF16)

    zero_b = (jnp.zeros((K, TILE), F32), jnp.zeros((C, TILE), F32))

    def own_rows(s, carry):
        def body(r, c):
            e3, e3b, e2 = errors(s, r)
            e3m[s, r - RIM] = e3b[:, :width]
            em = e2 * own_lane
            m = spread(em)
            e2m[s, r - RIM] = m
            if s == 0:
                up[r] = dot(w2t, m)
            else:
                up[r] = dot(w2t, spread(e2))
            return (c[0] + fold(e3[:, :width]), c[1] + fold(e2[:, :width]))

        return lax.fori_loop(RIM, RIM + h, body, carry, unroll=2)

    def rim_row(r):
        _, _, e2 = errors(1, r)
        up[r] = dot(w2t, spread(e2))

    def first_error(s, r):
        hid = up[r + 1][0:C] + up[r][C : 2 * C] + up[r - 1][2 * C :]
        z = z1[s, r]
        g = sigmoid(z)
        return hid * (g * (1.0 + z * (1.0 - g))) * inside(r)

    sums = own_rows(1, zero_b)
    for r in (RIM - 2, RIM - 1, RIM + h, RIM + h + 1):
        rim_row(r)

    def back_one(r, c):
        e1 = first_error(1, r)
        eb = e1.astype(BF16)
        e1m[1, r - RIM + 1] = (e1 * own_lane).astype(BF16)
        t = dot(w1t, eb)
        piece = lambda a, b: t[(3 * a + b) * LEV : (3 * a + b + 1) * LEV]
        for a in range(3):
            vv[r, a] = roll(piece(a, 0), -1) + piece(a, 1) + roll(piece(a, 2), 1)
        keep = jnp.where((r >= RIM) & (r < RIM + h), 1.0, 0.0).astype(F32)
        return c + fold(e1[:, :width]) * keep

    sum_one = lax.fori_loop(
        RIM - 1, RIM + h + 1, back_one, jnp.zeros((C, TILE), F32), unroll=2
    )

    def adjoint_next(r):
        wg = wet_s[r] * adj[1, r]
        p = prob[1, r]
        c = [0.25 * p[n * 8 : n * 8 + 8] for n in range(4)]
        above = wet_s[r - 1] * adj[1, r - 1] * (0.25 * prob[1, r - 1][0:8])
        below = wet_s[r + 1] * adj[1, r + 1] * (0.25 * prob[1, r + 1][8:16])
        adj[0, r] = (
            adj[1, r]
            - wg * (c[0] + c[1] + c[2] + c[3])
            + above
            + below
            + roll(wg * c[2], 1)
            + roll(wg * c[3], -1)
            + vv[r + 1, 0]
            + vv[r, 1]
            + vv[r - 1, 2]
        )

    loop(RIM, RIM + h, adjoint_next, 1)

    sums = own_rows(0, sums)
    for r in (RIM - 2, RIM - 1, RIM + h, RIM + h + 1):
        up[r] = jnp.zeros((3 * C, wide), F32)

    def back_zero(r, c):
        e1 = first_error(0, r)
        e1m[0, r - RIM + 1] = e1.astype(BF16)
        return c + fold(e1)

    sum_one = lax.fori_loop(RIM - 1, RIM + h + 1, back_zero, sum_one, unroll=2)

    g1 = jnp.zeros((C, 9 * LEV), F32)
    g2 = jnp.zeros((3 * C, 3 * C), F32)
    g3 = jnp.zeros((K, C), F32)
    for s in range(2):
        for r in range(h):
            h3 = jnp.concatenate([h1[s, RIM + r + a - 1] for a in range(3)], axis=0)
            g2 = g2 + dot_nt(e2m[s, r], h3)
            g3 = g3 + dot_nt(e3m[s, r], h2[s, RIM + r][:, :width])
        for r in range(h + 2) if s == 0 else range(1, h + 1):
            g1 = g1 + dot_nt(e1m[s, r], x9[s, RIM + r - 1])
    total = lambda v: jnp.sum(v, axis=1, keepdims=True)
    pad = lambda v: jnp.concatenate([v, jnp.zeros((v.shape[0], C - v.shape[1]), F32)], axis=1)
    extra = jnp.concatenate(
        [
            g1[:, :C],
            pad(jnp.concatenate([g1[:, C:], total(sum_one), total(sums[1])], axis=1)),
            g3,
            pad(total(sums[0])),
        ],
        axis=0,
    )
    grads_ref[: 3 * C, :] = jnp.concatenate([g2, extra], axis=1)
    spare = grads_ref.shape[0] - 3 * C
    if spare:
        grads_ref[3 * C :, :] = jnp.zeros((spare, 4 * C), F32)


def sum_kernel(sizes, grads, out, got, part, parts, send_one, recv_one, send_two, recv_two,
               send_three, recv_three):
    n_gx, n_gy = sizes
    gx = lax.axis_index("gx")
    gy = lax.axis_index("gy")
    chunk = grads.shape[0] // n_gy
    barrier = pltpu.get_barrier_semaphore()
    ys = [lax.rem(gy + k, n_gy) for k in range(1, n_gy)]
    xs = [lax.rem(gx + k, n_gx) for k in range(1, n_gx)]
    for y in ys:
        pl.semaphore_signal(barrier, inc=1, device_id=(gx, y), device_id_type=MESH)
    for x in xs:
        pl.semaphore_signal(barrier, inc=1, device_id=(x, gy), device_id_type=MESH)
    pl.semaphore_wait(barrier, n_gy + n_gx - 2)

    def rows(y):
        return pl.ds(pl.multiple_of(y * chunk, 8), chunk)

    one = [
        pltpu.make_async_remote_copy(
            src_ref=grads.at[rows(y)], dst_ref=got.at[k],
            send_sem=send_one.at[k], recv_sem=recv_one.at[k],
            device_id=(gx, y), device_id_type=MESH,
        )
        for k, y in enumerate(ys)
    ]
    for copy in one:
        copy.start()
    acc = grads[rows(gy), :]
    for k, copy in enumerate(one):
        copy.wait_recv()
        acc = acc + got[k]
    part[...] = acc
    two = [
        pltpu.make_async_remote_copy(
            src_ref=part, dst_ref=parts.at[gx],
            send_sem=send_two.at[k], recv_sem=recv_two.at[k],
            device_id=(x, gy), device_id_type=MESH,
        )
        for k, x in enumerate(xs)
    ]
    for copy in two:
        copy.start()
    parts[gx] = acc
    for copy in two:
        copy.wait_recv()
    acc = parts[0]
    for x in range(1, n_gx):
        acc = acc + parts[x]
    out[rows(gy), :] = acc
    three = [
        pltpu.make_async_remote_copy(
            src_ref=out.at[rows(gy)], dst_ref=out.at[rows(gy)],
            send_sem=send_three.at[k], recv_sem=recv_three.at[k],
            device_id=(gx, y), device_id_type=MESH,
        )
        for k, y in enumerate(ys)
    ]
    for copy in three:
        copy.start()
    for copy in three:
        copy.wait_recv()
    for copy in one + two + three:
        copy.wait_send()


def finish_kernel(grads, d1, d2, d3, ids, u1, u2, u3):
    g = grads[: 3 * C, :]
    block = lambda a, b: g[b * C : (b + 1) * C, a * C : (a + 1) * C]
    side = g[:, 3 * C :]
    one = jnp.concatenate([side[:C], side[C : 2 * C, : 9 * LEV - C + 1]], axis=1)
    bias_two = side[C : 2 * C, 9 * LEV - C + 1 : 9 * LEV - C + 2]
    two = jnp.concatenate([block(a, b) for a in range(3) for b in range(3)] + [bias_two], axis=1)
    three = jnp.concatenate([side[2 * C : 2 * C + K], side[2 * C + K :, 0:1]], axis=1)
    members = [one, two, three]
    heads = [d1[...], d2[...], d3[...]]
    row_sq = lambda v: jnp.sum(v * v, axis=1, keepdims=True)
    grad_rows = jnp.concatenate([row_sq(m) for m in members], axis=0)
    dir_rows = jnp.concatenate([row_sq(m) for m in heads], axis=0)
    total = jnp.sum(grad_rows, axis=0, keepdims=True)
    factor = 1.0 / jnp.maximum(jnp.sqrt(total), 1.0)
    clip_rows = grad_rows * (factor * factor)
    count = grad_rows.shape[0]
    i0 = lax.broadcasted_iota(jnp.int32, (count, count), 0)
    i1 = lax.broadcasted_iota(jnp.int32, (count, count), 1)
    spread = jnp.broadcast_to(ids[...].astype(F32), (count, count))
    column = jnp.sum(jnp.where(i0 == i1, spread, 0.0), axis=1, keepdims=True)
    row_ratio = jnp.zeros((count, 1), F32)
    for k in range(GROUPS):
        hit = column == float(k)
        pick = lambda v: jnp.sum(jnp.where(hit, v, 0.0), axis=0, keepdims=True)
        ratio = jnp.sqrt(pick(clip_rows)) / jnp.sqrt(pick(dir_rows) + 1e-06)
        row_ratio = row_ratio + jnp.where(hit, ratio, 0.0)
    scaling = math.sqrt(PARAMS)
    start = 0
    for ref, member, head in zip((u1, u2, u3), members, heads):
        n = member.shape[0]
        ref[...] = scaling * (member * factor + row_ratio[start : start + n] * head)
        start += n


def per_device(sizes, field, target, mask, conv_one, conv_two, head, d1, d2, d3, ids):
    n_gx, n_gy = sizes
    _, h, width = field.shape
    rows = h + 2 * RIM
    wide = width + TILE
    shape = jax.ShapeDtypeStruct
    chunk = 8 * -(-3 * C // (8 * n_gy))
    own, left, right = pl.pallas_call(
        functools.partial(halo_kernel, sizes),
        name="halo",
        out_shape=[
            shape((rows, 24, width), F32),
            shape((rows, 24, TILE), F32),
            shape((rows, 24, TILE), F32),
        ],
        in_specs=[VM] * 3,
        out_specs=[VM] * 3,
        scratch_shapes=[pltpu.SemaphoreType.DMA((8,)), pltpu.SemaphoreType.DMA((8,))],
        compiler_params=pltpu.CompilerParams(collective_id=0, has_side_effects=True),
    )(field, target, mask)
    final, grads = pl.pallas_call(
        functools.partial(compute_kernel, sizes),
        name="local",
        out_shape=[shape(field.shape, F32), shape((chunk * n_gy, 4 * C), F32)],
        in_specs=[VM] * 6,
        out_specs=[VM] * 2,
        scratch_shapes=[
            pltpu.VMEM((3, rows, LEV, wide), F32),
            pltpu.VMEM((rows, LEV, wide), F32),
            pltpu.VMEM((rows, LEV, wide), F32),
            pltpu.VMEM((2, rows, LEV, wide), F32),
            pltpu.VMEM((2, rows, 9 * LEV, wide), BF16),
            pltpu.VMEM((2, rows, C, wide), F32),
            pltpu.VMEM((2, rows, C, wide), BF16),
            pltpu.VMEM((2, rows, C, wide), F32),
            pltpu.VMEM((2, rows, C, wide), BF16),
            pltpu.VMEM((2, rows, K, wide), F32),
            pltpu.VMEM((2, h, 3 * C, wide), BF16),
            pltpu.VMEM((rows, 3 * C, wide), F32),
            pltpu.VMEM((2, h + 2, C, wide), BF16),
            pltpu.VMEM((rows, 3, LEV, wide), F32),
            pltpu.VMEM((2, h, K, width), BF16),
        ],
        compiler_params=pltpu.CompilerParams(vmem_limit_bytes=LIMIT),
    )(own, left, right, conv_one, conv_two, head)
    dma = pltpu.SemaphoreType.DMA
    summed = pl.pallas_call(
        functools.partial(sum_kernel, sizes),
        name="gradsum",
        out_shape=shape(grads.shape, F32),
        in_specs=[VM],
        out_specs=VM,
        scratch_shapes=[
            pltpu.VMEM((n_gy - 1, chunk, 4 * C), F32),
            pltpu.VMEM((chunk, 4 * C), F32),
            pltpu.VMEM((n_gx, chunk, 4 * C), F32),
            dma((n_gy - 1,)), dma((n_gy - 1,)),
            dma((n_gx - 1,)), dma((n_gx - 1,)),
            dma((n_gy - 1,)), dma((n_gy - 1,)),
        ],
        compiler_params=pltpu.CompilerParams(collective_id=1, has_side_effects=True),
    )(grads)
    u1, u2, u3 = pl.pallas_call(
        finish_kernel,
        name="update",
        out_shape=[shape(conv_one.shape, F32), shape(conv_two.shape, F32), shape(head.shape, F32)],
        in_specs=[VM] * 5,
        out_specs=[VM] * 3,
    )(summed, d1, d2, d3, ids.reshape(1, -1))
    return final, u1, u2, u3


def solution(mesh):
    grid = P(None, "gx", "gy")
    placed = (grid, grid, P("gx", "gy")) + (P(),) * 7
    return jax.shard_map(
        functools.partial(per_device, (mesh.shape["gx"], mesh.shape["gy"])),
        mesh=mesh,
        in_specs=placed,
        out_specs=(grid, P(), P(), P()),
        check_vma=False,
    )
```

```python
import functools
import math

import jax
import jax.numpy as jnp
from jax import lax
from jax.experimental import pallas as pl
from jax.experimental.pallas import tpu as pltpu
from jax.sharding import PartitionSpec as P

GROUPS = 6
PARAMS = 43680
RIM = 6
NEAR = 2
LEV = 8
C = 64
K = 32
TILE = 128
MESH = pl.DeviceIdType.MESH
F32 = jnp.float32
BF16 = jnp.bfloat16
VM = pl.BlockSpec(memory_space=pltpu.VMEM)
LIMIT = 56 * 1024 * 1024
NT = (((1,), (1,)), ((), ()))


def dot(a, b):
    return jnp.dot(a, b, preferred_element_type=F32)


def dot_nt(a, b):
    return lax.dot_general(a, b, NT, preferred_element_type=F32)


def sigmoid(v):
    return 0.5 * jnp.tanh(0.5 * v) + 0.5


def halo_kernel(sizes, field, target, mask, fld, tgt, wet, left, right, packed, send_sem, recv_sem):
    n_gx, n_gy = sizes
    gx = lax.axis_index("gx")
    gy = lax.axis_index("gy")
    h, width = mask.shape
    lane = lax.broadcasted_iota(jnp.int32, (3 * LEV, TILE), 1)
    strips = [jnp.zeros((3 * LEV, TILE), F32) for _ in range(2)]
    for r in range(h):
        wide_wet = jnp.broadcast_to(mask[r : r + 1, :].astype(F32), (LEV, width))
        values = wide_wet * field[:, r, :]
        goal = target[:, r, :]
        fld[RIM + r] = values
        tgt[NEAR + r] = goal
        rows = jnp.concatenate([values, wide_wet, goal], axis=0)
        here = (lane >= LEV * r) & (lane < LEV * r + LEV)
        low = rows[:, :TILE]
        high = rows[:, width - TILE :]
        strips[0] = jnp.where(here, roll(high, LEV * r + LEV), strips[0])
        strips[1] = jnp.where(here, roll(low, LEV * r), strips[1])
    wet[1] = mask[...].astype(F32)
    packed[0] = strips[0]
    packed[1] = strips[1]

    moves = [(dx, dy) for dx in (-1, 0, 1) for dy in (-1, 0, 1) if (dx, dy) != (0, 0)]

    def exists(dx, dy):
        x = gx + dx
        y = gy + dy
        return (x >= 0) & (x < n_gx) & (y >= 0) & (y < n_gy)

    def pairs(dx, dy):
        if dy:
            side = left if dy > 0 else right
            return [(packed.at[0 if dy > 0 else 1], side.at[1 - dx])]
        if dx > 0:
            return [
                (fld.at[pl.ds(h, RIM)], fld.at[pl.ds(0, RIM)]),
                (tgt.at[pl.ds(h, NEAR)], tgt.at[pl.ds(0, NEAR)]),
                (wet.at[1], wet.at[0]),
            ]
        return [
            (fld.at[pl.ds(RIM, RIM)], fld.at[pl.ds(RIM + h, RIM)]),
            (tgt.at[pl.ds(NEAR, NEAR)], tgt.at[pl.ds(NEAR + h, NEAR)]),
            (wet.at[1], wet.at[2]),
        ]

    barrier = pltpu.get_barrier_semaphore()
    count = jnp.int32(0)
    for dx, dy in moves:
        @pl.when(exists(dx, dy))
        def _():
            pl.semaphore_signal(barrier, inc=1, device_id=(gx + dx, gy + dy), device_id_type=MESH)
        count = count + jnp.where(exists(dx, dy), 1, 0)
    for dx, dy in moves:
        @pl.when(jnp.logical_not(exists(-dx, -dy)))
        def _():
            for _, dst in pairs(dx, dy):
                dst[...] = jnp.zeros(dst.shape, F32)
    pl.semaphore_wait(barrier, count)

    copies = []
    index = 0
    for dx, dy in moves:
        group = []
        for src, dst in pairs(dx, dy):
            group.append(
                pltpu.make_async_remote_copy(
                    src_ref=src,
                    dst_ref=dst,
                    send_sem=send_sem.at[index],
                    recv_sem=recv_sem.at[index],
                    device_id=(gx + dx, gy + dy),
                    device_id_type=MESH,
                )
            )
            index += 1
        copies.append((dx, dy, group))
    for dx, dy, group in copies:
        @pl.when(exists(dx, dy))
        def _():
            for copy in group:
                copy.start()
    for dx, dy, group in copies:
        @pl.when(exists(-dx, -dy))
        def _():
            for copy in group:
                copy.wait_recv()
    for dx, dy, group in copies:
        @pl.when(exists(dx, dy))
        def _():
            for copy in group:
                copy.wait_send()


def roll(v, shift):
    return pltpu.roll(v, shift % v.shape[1], 1)


def compute_kernel(
    sizes, own, goal, mask, left, right, w1_ref, w2_ref, w3_ref,
    final_ref, grads_ref,
    fld, wet_s, tgt, adj, x9, z1, h1, z2, h2, prob, e2m, up, e1m, vv, e3m,
):
    n_gx, n_gy = sizes
    gx = lax.axis_index("gx")
    gy = lax.axis_index("gy")
    rows, _, width = own.shape
    h = rows - 2 * RIM
    wide = width + TILE

    is_right = lax.broadcasted_iota(jnp.int32, (3 * LEV, TILE), 1) < TILE // 2

    for r in range(rows):
        where = 0 if r < RIM else 1 if r < RIM + h else 2
        k = (r + h - RIM) % h
        rest = jnp.where(
            is_right, roll(right[where], -LEV * k), roll(left[where], -LEV * k - LEV)
        )
        fld[0, r] = jnp.concatenate([own[r], rest[:LEV]], axis=1)
        wet_row = jnp.broadcast_to(mask[where, k : k + 1, :], (LEV, width))
        wet_s[r] = jnp.concatenate([wet_row, rest[LEV : 2 * LEV]], axis=1)
        if RIM - NEAR <= r < RIM + h + NEAR:
            tgt[r] = jnp.concatenate([goal[r - RIM + NEAR], rest[2 * LEV :]], axis=1)

    wa = w1_ref[...]
    w1 = wa[:, : 9 * LEV].astype(BF16)
    b1 = wa[:, 9 * LEV :]
    wb = w2_ref[...]
    tap = lambda a, b: wb[:, (3 * a + b) * C : (3 * a + b + 1) * C]
    w2f = jnp.concatenate(
        [jnp.concatenate([tap(a, b) for a in range(3)], axis=1) for b in range(3)], axis=0
    )
    w2 = w2f.astype(BF16)
    w2t = w2f.T.astype(BF16)
    b2 = wb[:, 9 * C :]
    wc = w3_ref[...]
    w3 = wc[:, :C].astype(BF16)
    w3t = wc[:, :C].T.astype(BF16)
    b3 = wc[:, C:]
    w1t = wa[:, : 9 * LEV].T.astype(BF16)

    col_left = jnp.where(gy > 0, 1.0, 0.0).astype(F32)
    col_right = jnp.where(gy < n_gy - 1, 1.0, 0.0).astype(F32)
    side = jnp.where(is_right[0:1], col_right, col_left)
    col_ok = jnp.concatenate([jnp.ones((1, width), F32), side], axis=1)

    def inside(r):
        i = gx * h + r - RIM
        ok = (i >= 0) & (i < n_gx * h)
        return col_ok * jnp.where(ok, 1.0, 0.0).astype(F32)

    def loop(start, stop, body):
        lax.fori_loop(start, stop, lambda r, c: (body(r), c)[1], 0, unroll=True)

    def forward(s, rad):
        def first(r):
            parts = []
            for a in range(3):
                row = fld[s, r + a - 1]
                parts += [roll(row, 1), row, roll(row, -1)]
            cols = jnp.concatenate(parts, axis=0).astype(BF16)
            x9[s, r] = cols
            z = dot(w1, cols) + b1
            z1[s, r] = z
            h1[s, r] = (z * sigmoid(z) * inside(r)).astype(BF16)

        loop(RIM - rad - 1, RIM + h + rad + 1, first)

        def second(r):
            h3 = jnp.concatenate([h1[s, r - 1], h1[s, r], h1[s, r + 1]], axis=0)
            y = dot(w2, h3)
            z = roll(y[0:C], 1) + y[C : 2 * C] + roll(y[2 * C :], -1) + b2
            z2[s, r] = z
            hb = (z * sigmoid(z)).astype(BF16)
            h2[s, r] = hb
            p = sigmoid(dot(w3, hb) + b3)
            prob[s, r] = p
            center = fld[s, r]
            c = 0.25 * p
            change = (
                c[0:8] * (fld[s, r + 1] - center)
                + c[8:16] * (fld[s, r - 1] - center)
                + c[16:24] * (roll(center, -1) - center)
                + c[24:32] * (roll(center, 1) - center)
            )
            fld[s + 1, r] = center + wet_s[r] * change

        loop(RIM - rad, RIM + h + rad, second)

    forward(0, 4)
    forward(1, 2)
    for r in range(h):
        final_ref[:, r, :] = fld[2, RIM + r][:, :width]

    def adjoint_start(r):
        adj[1, r] = wet_s[r] * (fld[2, r] - tgt[r])

    loop(RIM - 2, RIM + h + 2, adjoint_start)

    lane_w = lax.broadcasted_iota(jnp.int32, (1, wide), 1)
    own_lane = jnp.where(lane_w < width, 1.0, 0.0).astype(F32)
    fold = lambda v: sum(v[:, k * TILE : (k + 1) * TILE] for k in range(v.shape[1] // TILE))

    def errors(s, r):
        center = fld[s, r]
        wg = wet_s[r] * adj[s, r]
        p = prob[s, r]
        diff = jnp.concatenate(
            [
                wg * (fld[s, r + 1] - center),
                wg * (fld[s, r - 1] - center),
                wg * (roll(center, -1) - center),
                wg * (roll(center, 1) - center),
            ],
            axis=0,
        )
        e3 = diff * (0.25 * p * (1.0 - p))
        e3b = e3.astype(BF16)
        z = z2[s, r]
        g = sigmoid(z)
        e2 = dot(w3t, e3b) * (g * (1.0 + z * (1.0 - g)))
        return e3, e3b, e2

    def spread(e2):
        return jnp.concatenate([roll(e2, -1), e2, roll(e2, 1)], axis=0).astype(BF16)

    zero_b = (jnp.zeros((K, TILE), F32), jnp.zeros((C, TILE), F32))

    def own_rows(s, carry):
        def body(r, c):
            e3, e3b, e2 = errors(s, r)
            e3m[s, r - RIM] = e3b[:, :width]
            em = e2 * own_lane
            m = spread(em)
            e2m[s, r - RIM] = m
            if s == 0:
                up[r] = dot(w2t, m)
            else:
                up[r] = dot(w2t, spread(e2))
            return (c[0] + fold(e3[:, :width]), c[1] + fold(e2[:, :width]))

        return lax.fori_loop(RIM, RIM + h, body, carry, unroll=True)

    def rim_row(r):
        _, _, e2 = errors(1, r)
        up[r] = dot(w2t, spread(e2))

    def first_error(s, r):
        hid = up[r + 1][0:C] + up[r][C : 2 * C] + up[r - 1][2 * C :]
        z = z1[s, r]
        g = sigmoid(z)
        return hid * (g * (1.0 + z * (1.0 - g))) * inside(r)

    sums = own_rows(1, zero_b)
    for r in (RIM - 2, RIM - 1, RIM + h, RIM + h + 1):
        rim_row(r)

    def back_one(r, c):
        e1 = first_error(1, r)
        eb = e1.astype(BF16)
        e1m[1, r - RIM + 1] = (e1 * own_lane).astype(BF16)
        t = dot(w1t, eb)
        piece = lambda a, b: t[(3 * a + b) * LEV : (3 * a + b + 1) * LEV]
        for a in range(3):
            vv[r, a] = roll(piece(a, 0), -1) + piece(a, 1) + roll(piece(a, 2), 1)
        keep = jnp.where((r >= RIM) & (r < RIM + h), 1.0, 0.0).astype(F32)
        return c + fold(e1[:, :width]) * keep

    sum_one = lax.fori_loop(
        RIM - 1, RIM + h + 1, back_one, jnp.zeros((C, TILE), F32), unroll=True
    )

    def adjoint_next(r):
        wg = wet_s[r] * adj[1, r]
        p = prob[1, r]
        c = [0.25 * p[n * 8 : n * 8 + 8] for n in range(4)]
        above = wet_s[r - 1] * adj[1, r - 1] * (0.25 * prob[1, r - 1][0:8])
        below = wet_s[r + 1] * adj[1, r + 1] * (0.25 * prob[1, r + 1][8:16])
        adj[0, r] = (
            adj[1, r]
            - wg * (c[0] + c[1] + c[2] + c[3])
            + above
            + below
            + roll(wg * c[2], 1)
            + roll(wg * c[3], -1)
            + vv[r + 1, 0]
            + vv[r, 1]
            + vv[r - 1, 2]
        )

    loop(RIM, RIM + h, adjoint_next)

    sums = own_rows(0, sums)
    for r in (RIM - 2, RIM - 1, RIM + h, RIM + h + 1):
        up[r] = jnp.zeros((3 * C, wide), F32)

    def back_zero(r, c):
        e1 = first_error(0, r)
        e1m[0, r - RIM + 1] = e1.astype(BF16)
        return c + fold(e1)

    sum_one = lax.fori_loop(RIM - 1, RIM + h + 1, back_zero, sum_one, unroll=True)

    g1 = jnp.zeros((C, 9 * LEV), F32)
    g2 = jnp.zeros((3 * C, 3 * C), F32)
    g3 = jnp.zeros((K, C), F32)
    for s in range(2):
        for r in range(h):
            h3 = jnp.concatenate([h1[s, RIM + r + a - 1] for a in range(3)], axis=0)
            g2 = g2 + dot_nt(e2m[s, r], h3)
            g3 = g3 + dot_nt(e3m[s, r], h2[s, RIM + r][:, :width])
        for r in range(h + 2) if s == 0 else range(1, h + 1):
            g1 = g1 + dot_nt(e1m[s, r], x9[s, RIM + r - 1])
    total = lambda v: jnp.sum(v, axis=1, keepdims=True)
    pad = lambda v: jnp.concatenate([v, jnp.zeros((v.shape[0], C - v.shape[1]), F32)], axis=1)
    extra = jnp.concatenate(
        [
            g1[:, :C],
            pad(jnp.concatenate([g1[:, C:], total(sum_one), total(sums[1])], axis=1)),
            g3,
            pad(total(sums[0])),
        ],
        axis=0,
    )
    grads_ref[: 3 * C, :] = jnp.concatenate([g2, extra], axis=1)
    spare = grads_ref.shape[0] - 3 * C
    if spare:
        grads_ref[3 * C :, :] = jnp.zeros((spare, 4 * C), F32)


def sum_kernel(sizes, grads, out, got, part, parts, send_one, recv_one, send_two, recv_two,
               send_three, recv_three):
    n_gx, n_gy = sizes
    gx = lax.axis_index("gx")
    gy = lax.axis_index("gy")
    chunk = grads.shape[0] // n_gy
    barrier = pltpu.get_barrier_semaphore()
    ys = [lax.rem(gy + k, n_gy) for k in range(1, n_gy)]
    xs = [lax.rem(gx + k, n_gx) for k in range(1, n_gx)]
    for y in ys:
        pl.semaphore_signal(barrier, inc=1, device_id=(gx, y), device_id_type=MESH)
    for x in xs:
        pl.semaphore_signal(barrier, inc=1, device_id=(x, gy), device_id_type=MESH)
    pl.semaphore_wait(barrier, n_gy + n_gx - 2)

    def rows(y):
        return pl.ds(pl.multiple_of(y * chunk, 8), chunk)

    one = [
        pltpu.make_async_remote_copy(
            src_ref=grads.at[rows(y)], dst_ref=got.at[k],
            send_sem=send_one.at[k], recv_sem=recv_one.at[k],
            device_id=(gx, y), device_id_type=MESH,
        )
        for k, y in enumerate(ys)
    ]
    for copy in one:
        copy.start()
    acc = grads[rows(gy), :]
    for k, copy in enumerate(one):
        copy.wait_recv()
        acc = acc + got[k]
    part[...] = acc
    two = [
        pltpu.make_async_remote_copy(
            src_ref=part, dst_ref=parts.at[gx],
            send_sem=send_two.at[k], recv_sem=recv_two.at[k],
            device_id=(x, gy), device_id_type=MESH,
        )
        for k, x in enumerate(xs)
    ]
    for copy in two:
        copy.start()
    parts[gx] = acc
    for copy in two:
        copy.wait_recv()
    acc = parts[0]
    for x in range(1, n_gx):
        acc = acc + parts[x]
    out[rows(gy), :] = acc
    three = [
        pltpu.make_async_remote_copy(
            src_ref=out.at[rows(gy)], dst_ref=out.at[rows(gy)],
            send_sem=send_three.at[k], recv_sem=recv_three.at[k],
            device_id=(gx, y), device_id_type=MESH,
        )
        for k, y in enumerate(ys)
    ]
    for copy in three:
        copy.start()
    for copy in three:
        copy.wait_recv()
    for copy in one + two + three:
        copy.wait_send()


def finish_kernel(grads, d1, d2, d3, ids, u1, u2, u3):
    g = grads[: 3 * C, :]
    block = lambda a, b: g[b * C : (b + 1) * C, a * C : (a + 1) * C]
    side = g[:, 3 * C :]
    one = jnp.concatenate([side[:C], side[C : 2 * C, : 9 * LEV - C + 1]], axis=1)
    bias_two = side[C : 2 * C, 9 * LEV - C + 1 : 9 * LEV - C + 2]
    two = jnp.concatenate([block(a, b) for a in range(3) for b in range(3)] + [bias_two], axis=1)
    three = jnp.concatenate([side[2 * C : 2 * C + K], side[2 * C + K :, 0:1]], axis=1)
    members = [one, two, three]
    heads = [d1[...], d2[...], d3[...]]
    row_sq = lambda v: jnp.sum(v * v, axis=1, keepdims=True)
    grad_rows = jnp.concatenate([row_sq(m) for m in members], axis=0)
    dir_rows = jnp.concatenate([row_sq(m) for m in heads], axis=0)
    total = jnp.sum(grad_rows, axis=0, keepdims=True)
    factor = 1.0 / jnp.maximum(jnp.sqrt(total), 1.0)
    clip_rows = grad_rows * (factor * factor)
    count = grad_rows.shape[0]
    i0 = lax.broadcasted_iota(jnp.int32, (count, count), 0)
    i1 = lax.broadcasted_iota(jnp.int32, (count, count), 1)
    spread = jnp.broadcast_to(ids[...].astype(F32), (count, count))
    column = jnp.sum(jnp.where(i0 == i1, spread, 0.0), axis=1, keepdims=True)
    row_ratio = jnp.zeros((count, 1), F32)
    for k in range(GROUPS):
        hit = column == float(k)
        pick = lambda v: jnp.sum(jnp.where(hit, v, 0.0), axis=0, keepdims=True)
        ratio = jnp.sqrt(pick(clip_rows)) / jnp.sqrt(pick(dir_rows) + 1e-06)
        row_ratio = row_ratio + jnp.where(hit, ratio, 0.0)
    scaling = math.sqrt(PARAMS)
    start = 0
    for ref, member, head in zip((u1, u2, u3), members, heads):
        n = member.shape[0]
        ref[...] = scaling * (member * factor + row_ratio[start : start + n] * head)
        start += n


def per_device(sizes, field, target, mask, conv_one, conv_two, head, d1, d2, d3, ids):
    n_gx, n_gy = sizes
    _, h, width = field.shape
    rows = h + 2 * RIM
    wide = width + TILE
    shape = jax.ShapeDtypeStruct
    chunk = 8 * -(-3 * C // (8 * n_gy))
    own, goal, wet, left, right = pl.pallas_call(
        functools.partial(halo_kernel, sizes),
        name="halo",
        out_shape=[
            shape((rows, LEV, width), F32),
            shape((h + 2 * NEAR, LEV, width), F32),
            shape((3, h, width), F32),
            shape((3, 3 * LEV, TILE), F32),
            shape((3, 3 * LEV, TILE), F32),
        ],
        in_specs=[VM] * 3,
        out_specs=[VM] * 5,
        scratch_shapes=[
            pltpu.VMEM((2, 3 * LEV, TILE), F32),
            pltpu.SemaphoreType.DMA((12,)),
            pltpu.SemaphoreType.DMA((12,)),
        ],
        compiler_params=pltpu.CompilerParams(collective_id=0, has_side_effects=True),
    )(field, target, mask)
    final, grads = pl.pallas_call(
        functools.partial(compute_kernel, sizes),
        name="local",
        out_shape=[shape(field.shape, F32), shape((chunk * n_gy, 4 * C), F32)],
        in_specs=[VM] * 8,
        out_specs=[VM] * 2,
        scratch_shapes=[
            pltpu.VMEM((3, rows, LEV, wide), F32),
            pltpu.VMEM((rows, LEV, wide), F32),
            pltpu.VMEM((rows, LEV, wide), F32),
            pltpu.VMEM((2, rows, LEV, wide), F32),
            pltpu.VMEM((2, rows, 9 * LEV, wide), BF16),
            pltpu.VMEM((2, rows, C, wide), F32),
            pltpu.VMEM((2, rows, C, wide), BF16),
            pltpu.VMEM((2, rows, C, wide), F32),
            pltpu.VMEM((2, rows, C, wide), BF16),
            pltpu.VMEM((2, rows, K, wide), F32),
            pltpu.VMEM((2, h, 3 * C, wide), BF16),
            pltpu.VMEM((rows, 3 * C, wide), F32),
            pltpu.VMEM((2, h + 2, C, wide), BF16),
            pltpu.VMEM((rows, 3, LEV, wide), F32),
            pltpu.VMEM((2, h, K, width), BF16),
        ],
        compiler_params=pltpu.CompilerParams(vmem_limit_bytes=LIMIT),
    )(own, goal, wet, left, right, conv_one, conv_two, head)
    dma = pltpu.SemaphoreType.DMA
    summed = pl.pallas_call(
        functools.partial(sum_kernel, sizes),
        name="gradsum",
        out_shape=shape(grads.shape, F32),
        in_specs=[VM],
        out_specs=VM,
        scratch_shapes=[
            pltpu.VMEM((n_gy - 1, chunk, 4 * C), F32),
            pltpu.VMEM((chunk, 4 * C), F32),
            pltpu.VMEM((n_gx, chunk, 4 * C), F32),
            dma((n_gy - 1,)), dma((n_gy - 1,)),
            dma((n_gx - 1,)), dma((n_gx - 1,)),
            dma((n_gy - 1,)), dma((n_gy - 1,)),
        ],
        compiler_params=pltpu.CompilerParams(collective_id=1, has_side_effects=True),
    )(grads)
    u1, u2, u3 = pl.pallas_call(
        finish_kernel,
        name="update",
        out_shape=[shape(conv_one.shape, F32), shape(conv_two.shape, F32), shape(head.shape, F32)],
        in_specs=[VM] * 5,
        out_specs=[VM] * 3,
    )(summed, d1, d2, d3, ids.reshape(1, -1))
    return final, u1, u2, u3


def solution(mesh):
    grid = P(None, "gx", "gy")
    placed = (grid, grid, P("gx", "gy")) + (P(),) * 7
    return jax.shard_map(
        functools.partial(per_device, (mesh.shape["gx"], mesh.shape["gy"])),
        mesh=mesh,
        in_specs=placed,
        out_specs=(grid, P(), P(), P()),
        check_vma=False,
    )
```

```python
import functools
import math

import jax
import jax.numpy as jnp
from jax import lax
from jax.experimental import pallas as pl
from jax.experimental.pallas import tpu as pltpu
from jax.sharding import PartitionSpec as P

GROUPS = 6
PARAMS = 43680
RIM = 6
NEAR = 2
LEV = 8
C = 64
K = 32
TILE = 128
MESH = pl.DeviceIdType.MESH
F32 = jnp.float32
BF16 = jnp.bfloat16
VM = pl.BlockSpec(memory_space=pltpu.VMEM)
LIMIT = 56 * 1024 * 1024
NT = (((1,), (1,)), ((), ()))


def dot(a, b):
    return jnp.dot(a, b, preferred_element_type=F32)


def dot_nt(a, b):
    return lax.dot_general(a, b, NT, preferred_element_type=F32)


def sigmoid(v):
    return 0.5 * jnp.tanh(0.5 * v) + 0.5


def halo_kernel(sizes, field, target, mask, fld, tgt, wet, left, right, packed, send_sem, recv_sem):
    n_gx, n_gy = sizes
    gx = lax.axis_index("gx")
    gy = lax.axis_index("gy")
    h, width = mask.shape
    lane = lax.broadcasted_iota(jnp.int32, (3 * LEV, TILE), 1)
    strips = [jnp.zeros((3 * LEV, TILE), F32) for _ in range(2)]
    for r in range(h):
        wide_wet = jnp.broadcast_to(mask[r : r + 1, :].astype(F32), (LEV, width))
        values = wide_wet * field[:, r, :]
        goal = target[:, r, :]
        fld[RIM + r] = values
        tgt[NEAR + r] = goal
        rows = jnp.concatenate([values, wide_wet, goal], axis=0)
        here = (lane >= LEV * r) & (lane < LEV * r + LEV)
        low = rows[:, :TILE]
        high = rows[:, width - TILE :]
        strips[0] = jnp.where(here, roll(high, LEV * r + LEV), strips[0])
        strips[1] = jnp.where(here, roll(low, LEV * r), strips[1])
    wet[1] = mask[...].astype(F32)
    packed[0] = strips[0]
    packed[1] = strips[1]

    moves = [(dx, dy) for dx in (-1, 0, 1) for dy in (-1, 0, 1) if (dx, dy) != (0, 0)]

    def exists(dx, dy):
        x = gx + dx
        y = gy + dy
        return (x >= 0) & (x < n_gx) & (y >= 0) & (y < n_gy)

    def pairs(dx, dy):
        if dy:
            side = left if dy > 0 else right
            return [(packed.at[0 if dy > 0 else 1], side.at[1 - dx])]
        if dx > 0:
            return [
                (fld.at[pl.ds(h, RIM)], fld.at[pl.ds(0, RIM)]),
                (tgt.at[pl.ds(h, NEAR)], tgt.at[pl.ds(0, NEAR)]),
                (wet.at[1], wet.at[0]),
            ]
        return [
            (fld.at[pl.ds(RIM, RIM)], fld.at[pl.ds(RIM + h, RIM)]),
            (tgt.at[pl.ds(NEAR, NEAR)], tgt.at[pl.ds(NEAR + h, NEAR)]),
            (wet.at[1], wet.at[2]),
        ]

    barrier = pltpu.get_barrier_semaphore()
    count = jnp.int32(0)
    for dx, dy in moves:
        @pl.when(exists(dx, dy))
        def _():
            pl.semaphore_signal(barrier, inc=1, device_id=(gx + dx, gy + dy), device_id_type=MESH)
        count = count + jnp.where(exists(dx, dy), 1, 0)
    for dx, dy in moves:
        @pl.when(jnp.logical_not(exists(-dx, -dy)))
        def _():
            for _, dst in pairs(dx, dy):
                dst[...] = jnp.zeros(dst.shape, F32)
    pl.semaphore_wait(barrier, count)

    copies = []
    index = 0
    for dx, dy in moves:
        group = []
        for src, dst in pairs(dx, dy):
            group.append(
                pltpu.make_async_remote_copy(
                    src_ref=src,
                    dst_ref=dst,
                    send_sem=send_sem.at[index],
                    recv_sem=recv_sem.at[index],
                    device_id=(gx + dx, gy + dy),
                    device_id_type=MESH,
                )
            )
            index += 1
        copies.append((dx, dy, group))
    for dx, dy, group in copies:
        @pl.when(exists(dx, dy))
        def _():
            for copy in group:
                copy.start()
    for dx, dy, group in copies:
        @pl.when(exists(-dx, -dy))
        def _():
            for copy in group:
                copy.wait_recv()
    for dx, dy, group in copies:
        @pl.when(exists(dx, dy))
        def _():
            for copy in group:
                copy.wait_send()


def roll(v, shift):
    return pltpu.roll(v, shift % v.shape[1], 1)


def compute_kernel(
    sizes, own, goal, mask, left, right, w1_ref, w2_ref, w3_ref,
    final_ref, grads_ref,
    fld, wet_s, tgt, adj, x9, z1, h1, z2, h2, prob, e2m, up, e1m, vv, e3m,
):
    n_gx, n_gy = sizes
    gx = lax.axis_index("gx")
    gy = lax.axis_index("gy")
    rows, _, width = own.shape
    h = rows - 2 * RIM
    wide = width + TILE

    is_right = lax.broadcasted_iota(jnp.int32, (3 * LEV, TILE), 1) < TILE // 2

    for r in range(rows):
        where = 0 if r < RIM else 1 if r < RIM + h else 2
        k = (r + h - RIM) % h
        rest = jnp.where(
            is_right, roll(right[where], -LEV * k), roll(left[where], -LEV * k - LEV)
        )
        fld[0, r] = jnp.concatenate([own[r], rest[:LEV]], axis=1)
        wet_row = jnp.broadcast_to(mask[where, k : k + 1, :], (LEV, width))
        wet_s[r] = jnp.concatenate([wet_row, rest[LEV : 2 * LEV]], axis=1)
        if RIM - NEAR <= r < RIM + h + NEAR:
            tgt[r] = jnp.concatenate([goal[r - RIM + NEAR], rest[2 * LEV :]], axis=1)

    wa = w1_ref[...]
    w1 = wa[:, : 9 * LEV].astype(BF16)
    b1 = wa[:, 9 * LEV :]
    wb = w2_ref[...]
    tap = lambda a, b: wb[:, (3 * a + b) * C : (3 * a + b + 1) * C]
    w2f = jnp.concatenate(
        [jnp.concatenate([tap(a, b) for a in range(3)], axis=1) for b in range(3)], axis=0
    )
    w2 = w2f.astype(BF16)
    w2t = w2f.T.astype(BF16)
    b2 = wb[:, 9 * C :]
    wc = w3_ref[...]
    w3 = wc[:, :C].astype(BF16)
    w3t = wc[:, :C].T.astype(BF16)
    b3 = wc[:, C:]
    w1t = wa[:, : 9 * LEV].T.astype(BF16)

    col_left = jnp.where(gy > 0, 1.0, 0.0).astype(F32)
    col_right = jnp.where(gy < n_gy - 1, 1.0, 0.0).astype(F32)
    side = jnp.where(is_right[0:1], col_right, col_left)
    col_ok = jnp.concatenate([jnp.ones((1, width), F32), side], axis=1)

    def inside(r):
        i = gx * h + r - RIM
        ok = (i >= 0) & (i < n_gx * h)
        return col_ok * jnp.where(ok, 1.0, 0.0).astype(F32)

    def loop(start, stop, body):
        lax.fori_loop(start, stop, lambda r, c: (body(r), c)[1], 0, unroll=True)

    def forward(s, rad):
        def first(r):
            parts = []
            for a in range(3):
                row = fld[s, r + a - 1]
                parts += [roll(row, 1), row, roll(row, -1)]
            cols = jnp.concatenate(parts, axis=0).astype(BF16)
            x9[s, r] = cols
            z = dot(w1, cols) + b1
            z1[s, r] = z
            h1[s, r] = (z * sigmoid(z) * inside(r)).astype(BF16)


        def second(r):
            h3 = jnp.concatenate([h1[s, r - 1], h1[s, r], h1[s, r + 1]], axis=0)
            y = dot(w2, h3)
            z = roll(y[0:C], 1) + y[C : 2 * C] + roll(y[2 * C :], -1) + b2
            z2[s, r] = z
            hb = (z * sigmoid(z)).astype(BF16)
            h2[s, r] = hb
            p = sigmoid(dot(w3, hb) + b3)
            prob[s, r] = p
            center = fld[s, r]
            c = 0.25 * p
            change = (
                c[0:8] * (fld[s, r + 1] - center)
                + c[8:16] * (fld[s, r - 1] - center)
                + c[16:24] * (roll(center, -1) - center)
                + c[24:32] * (roll(center, 1) - center)
            )
            fld[s + 1, r] = center + wet_s[r] * change

        begin = RIM - rad
        first(begin - 1)
        first(begin)
        first(begin + 1)
        for r in range(begin, RIM + h + rad):
            if r + 2 <= RIM + h + rad:
                first(r + 2)
            second(r)

    forward(0, 4)
    forward(1, 2)
    for r in range(h):
        final_ref[:, r, :] = fld[2, RIM + r][:, :width]

    def adjoint_start(r):
        adj[1, r] = wet_s[r] * (fld[2, r] - tgt[r])

    loop(RIM - 2, RIM + h + 2, adjoint_start)

    lane_w = lax.broadcasted_iota(jnp.int32, (1, wide), 1)
    own_lane = jnp.where(lane_w < width, 1.0, 0.0).astype(F32)
    fold = lambda v: sum(v[:, k * TILE : (k + 1) * TILE] for k in range(v.shape[1] // TILE))

    def errors(s, r):
        center = fld[s, r]
        wg = wet_s[r] * adj[s, r]
        p = prob[s, r]
        diff = jnp.concatenate(
            [
                wg * (fld[s, r + 1] - center),
                wg * (fld[s, r - 1] - center),
                wg * (roll(center, -1) - center),
                wg * (roll(center, 1) - center),
            ],
            axis=0,
        )
        e3 = diff * (0.25 * p * (1.0 - p))
        e3b = e3.astype(BF16)
        z = z2[s, r]
        g = sigmoid(z)
        e2 = dot(w3t, e3b) * (g * (1.0 + z * (1.0 - g)))
        return e3, e3b, e2

    def spread(e2):
        return jnp.concatenate([roll(e2, -1), e2, roll(e2, 1)], axis=0).astype(BF16)

    zero_b = (jnp.zeros((K, TILE), F32), jnp.zeros((C, TILE), F32))

    def own_row(s):
        def body(r, c):
            e3, e3b, e2 = errors(s, r)
            e3m[s, r - RIM] = e3b[:, :width]
            em = e2 * own_lane
            m = spread(em)
            e2m[s, r - RIM] = m
            if s == 0:
                up[r] = dot(w2t, m)
            else:
                up[r] = dot(w2t, spread(e2))
            return (c[0] + fold(e3[:, :width]), c[1] + fold(e2[:, :width]))

        return body

    def rim_row(r):
        _, _, e2 = errors(1, r)
        up[r] = dot(w2t, spread(e2))

    def first_error(s, r):
        hid = up[r + 1][0:C] + up[r][C : 2 * C] + up[r - 1][2 * C :]
        z = z1[s, r]
        g = sigmoid(z)
        return hid * (g * (1.0 + z * (1.0 - g))) * inside(r)

    def back_one(r, c):
        e1 = first_error(1, r)
        eb = e1.astype(BF16)
        e1m[1, r - RIM + 1] = (e1 * own_lane).astype(BF16)
        t = dot(w1t, eb)
        piece = lambda a, b: t[(3 * a + b) * LEV : (3 * a + b + 1) * LEV]
        for a in range(3):
            vv[r, a] = roll(piece(a, 0), -1) + piece(a, 1) + roll(piece(a, 2), 1)
        return c + fold(e1[:, :width]) if RIM <= r < RIM + h else c

    def backward(rim, own_part, back, sums, sum_one):
        for r in range(RIM - 2, RIM + h + 2):
            if RIM <= r < RIM + h:
                sums = own_part(r, sums)
            else:
                rim(r)
            if r >= RIM:
                sum_one = back(r - 1, sum_one)
        return sums, sum_one

    sums, sum_one = backward(rim_row, own_row(1), back_one, zero_b, jnp.zeros((C, TILE), F32))

    def adjoint_next(r):
        wg = wet_s[r] * adj[1, r]
        p = prob[1, r]
        c = [0.25 * p[n * 8 : n * 8 + 8] for n in range(4)]
        above = wet_s[r - 1] * adj[1, r - 1] * (0.25 * prob[1, r - 1][0:8])
        below = wet_s[r + 1] * adj[1, r + 1] * (0.25 * prob[1, r + 1][8:16])
        adj[0, r] = (
            adj[1, r]
            - wg * (c[0] + c[1] + c[2] + c[3])
            + above
            + below
            + roll(wg * c[2], 1)
            + roll(wg * c[3], -1)
            + vv[r + 1, 0]
            + vv[r, 1]
            + vv[r - 1, 2]
        )

    loop(RIM, RIM + h, adjoint_next)

    def rim_zero(r):
        up[r] = jnp.zeros((3 * C, wide), F32)

    def back_zero(r, c):
        e1 = first_error(0, r)
        e1m[0, r - RIM + 1] = e1.astype(BF16)
        return c + fold(e1)

    sums, sum_one = backward(rim_zero, own_row(0), back_zero, sums, sum_one)

    g1 = jnp.zeros((C, 9 * LEV), F32)
    g2 = jnp.zeros((3 * C, 3 * C), F32)
    g3 = jnp.zeros((K, C), F32)
    for s in range(2):
        for r in range(h):
            h3 = jnp.concatenate([h1[s, RIM + r + a - 1] for a in range(3)], axis=0)
            g2 = g2 + dot_nt(e2m[s, r], h3)
            g3 = g3 + dot_nt(e3m[s, r], h2[s, RIM + r][:, :width])
        for r in range(h + 2) if s == 0 else range(1, h + 1):
            g1 = g1 + dot_nt(e1m[s, r], x9[s, RIM + r - 1])
    total = lambda v: jnp.sum(v, axis=1, keepdims=True)
    pad = lambda v: jnp.concatenate([v, jnp.zeros((v.shape[0], C - v.shape[1]), F32)], axis=1)
    extra = jnp.concatenate(
        [
            g1[:, :C],
            pad(jnp.concatenate([g1[:, C:], total(sum_one), total(sums[1])], axis=1)),
            g3,
            pad(total(sums[0])),
        ],
        axis=0,
    )
    grads_ref[: 3 * C, :] = jnp.concatenate([g2, extra], axis=1)
    spare = grads_ref.shape[0] - 3 * C
    if spare:
        grads_ref[3 * C :, :] = jnp.zeros((spare, 4 * C), F32)


def sum_kernel(sizes, grads, out, got, part, parts, send_one, recv_one, send_two, recv_two,
               send_three, recv_three):
    n_gx, n_gy = sizes
    gx = lax.axis_index("gx")
    gy = lax.axis_index("gy")
    chunk = grads.shape[0] // n_gy
    barrier = pltpu.get_barrier_semaphore()
    ys = [lax.rem(gy + k, n_gy) for k in range(1, n_gy)]
    xs = [lax.rem(gx + k, n_gx) for k in range(1, n_gx)]
    for y in ys:
        pl.semaphore_signal(barrier, inc=1, device_id=(gx, y), device_id_type=MESH)
    for x in xs:
        pl.semaphore_signal(barrier, inc=1, device_id=(x, gy), device_id_type=MESH)
    pl.semaphore_wait(barrier, n_gy + n_gx - 2)

    def rows(y):
        return pl.ds(pl.multiple_of(y * chunk, 8), chunk)

    one = [
        pltpu.make_async_remote_copy(
            src_ref=grads.at[rows(y)], dst_ref=got.at[k],
            send_sem=send_one.at[k], recv_sem=recv_one.at[k],
            device_id=(gx, y), device_id_type=MESH,
        )
        for k, y in enumerate(ys)
    ]
    for copy in one:
        copy.start()
    acc = grads[rows(gy), :]
    for k, copy in enumerate(one):
        copy.wait_recv()
        acc = acc + got[k]
    part[...] = acc
    two = [
        pltpu.make_async_remote_copy(
            src_ref=part, dst_ref=parts.at[gx],
            send_sem=send_two.at[k], recv_sem=recv_two.at[k],
            device_id=(x, gy), device_id_type=MESH,
        )
        for k, x in enumerate(xs)
    ]
    for copy in two:
        copy.start()
    parts[gx] = acc
    for copy in two:
        copy.wait_recv()
    acc = parts[0]
    for x in range(1, n_gx):
        acc = acc + parts[x]
    out[rows(gy), :] = acc
    three = [
        pltpu.make_async_remote_copy(
            src_ref=out.at[rows(gy)], dst_ref=out.at[rows(gy)],
            send_sem=send_three.at[k], recv_sem=recv_three.at[k],
            device_id=(gx, y), device_id_type=MESH,
        )
        for k, y in enumerate(ys)
    ]
    for copy in three:
        copy.start()
    for copy in three:
        copy.wait_recv()
    for copy in one + two + three:
        copy.wait_send()


def finish_kernel(grads, d1, d2, d3, ids, u1, u2, u3):
    g = grads[: 3 * C, :]
    block = lambda a, b: g[b * C : (b + 1) * C, a * C : (a + 1) * C]
    side = g[:, 3 * C :]
    one = jnp.concatenate([side[:C], side[C : 2 * C, : 9 * LEV - C + 1]], axis=1)
    bias_two = side[C : 2 * C, 9 * LEV - C + 1 : 9 * LEV - C + 2]
    two = jnp.concatenate([block(a, b) for a in range(3) for b in range(3)] + [bias_two], axis=1)
    three = jnp.concatenate([side[2 * C : 2 * C + K], side[2 * C + K :, 0:1]], axis=1)
    members = [one, two, three]
    heads = [d1[...], d2[...], d3[...]]
    row_sq = lambda v: jnp.sum(v * v, axis=1, keepdims=True)
    grad_rows = jnp.concatenate([row_sq(m) for m in members], axis=0)
    dir_rows = jnp.concatenate([row_sq(m) for m in heads], axis=0)
    total = jnp.sum(grad_rows, axis=0, keepdims=True)
    factor = 1.0 / jnp.maximum(jnp.sqrt(total), 1.0)
    clip_rows = grad_rows * (factor * factor)
    count = grad_rows.shape[0]
    i0 = lax.broadcasted_iota(jnp.int32, (count, count), 0)
    i1 = lax.broadcasted_iota(jnp.int32, (count, count), 1)
    spread = jnp.broadcast_to(ids[...].astype(F32), (count, count))
    column = jnp.sum(jnp.where(i0 == i1, spread, 0.0), axis=1, keepdims=True)
    row_ratio = jnp.zeros((count, 1), F32)
    for k in range(GROUPS):
        hit = column == float(k)
        pick = lambda v: jnp.sum(jnp.where(hit, v, 0.0), axis=0, keepdims=True)
        ratio = jnp.sqrt(pick(clip_rows)) / jnp.sqrt(pick(dir_rows) + 1e-06)
        row_ratio = row_ratio + jnp.where(hit, ratio, 0.0)
    scaling = math.sqrt(PARAMS)
    start = 0
    for ref, member, head in zip((u1, u2, u3), members, heads):
        n = member.shape[0]
        ref[...] = scaling * (member * factor + row_ratio[start : start + n] * head)
        start += n


def per_device(sizes, field, target, mask, conv_one, conv_two, head, d1, d2, d3, ids):
    n_gx, n_gy = sizes
    _, h, width = field.shape
    rows = h + 2 * RIM
    wide = width + TILE
    shape = jax.ShapeDtypeStruct
    chunk = 8 * -(-3 * C // (8 * n_gy))
    own, goal, wet, left, right = pl.pallas_call(
        functools.partial(halo_kernel, sizes),
        name="halo",
        out_shape=[
            shape((rows, LEV, width), F32),
            shape((h + 2 * NEAR, LEV, width), F32),
            shape((3, h, width), F32),
            shape((3, 3 * LEV, TILE), F32),
            shape((3, 3 * LEV, TILE), F32),
        ],
        in_specs=[VM] * 3,
        out_specs=[VM] * 5,
        scratch_shapes=[
            pltpu.VMEM((2, 3 * LEV, TILE), F32),
            pltpu.SemaphoreType.DMA((12,)),
            pltpu.SemaphoreType.DMA((12,)),
        ],
        compiler_params=pltpu.CompilerParams(collective_id=0, has_side_effects=True),
    )(field, target, mask)
    final, grads = pl.pallas_call(
        functools.partial(compute_kernel, sizes),
        name="local",
        out_shape=[shape(field.shape, F32), shape((chunk * n_gy, 4 * C), F32)],
        in_specs=[VM] * 8,
        out_specs=[VM] * 2,
        scratch_shapes=[
            pltpu.VMEM((3, rows, LEV, wide), F32),
            pltpu.VMEM((rows, LEV, wide), F32),
            pltpu.VMEM((rows, LEV, wide), F32),
            pltpu.VMEM((2, rows, LEV, wide), F32),
            pltpu.VMEM((2, rows, 9 * LEV, wide), BF16),
            pltpu.VMEM((2, rows, C, wide), F32),
            pltpu.VMEM((2, rows, C, wide), BF16),
            pltpu.VMEM((2, rows, C, wide), F32),
            pltpu.VMEM((2, rows, C, wide), BF16),
            pltpu.VMEM((2, rows, K, wide), F32),
            pltpu.VMEM((2, h, 3 * C, wide), BF16),
            pltpu.VMEM((rows, 3 * C, wide), F32),
            pltpu.VMEM((2, h + 2, C, wide), BF16),
            pltpu.VMEM((rows, 3, LEV, wide), F32),
            pltpu.VMEM((2, h, K, width), BF16),
        ],
        compiler_params=pltpu.CompilerParams(vmem_limit_bytes=LIMIT),
    )(own, goal, wet, left, right, conv_one, conv_two, head)
    dma = pltpu.SemaphoreType.DMA
    summed = pl.pallas_call(
        functools.partial(sum_kernel, sizes),
        name="gradsum",
        out_shape=shape(grads.shape, F32),
        in_specs=[VM],
        out_specs=VM,
        scratch_shapes=[
            pltpu.VMEM((n_gy - 1, chunk, 4 * C), F32),
            pltpu.VMEM((chunk, 4 * C), F32),
            pltpu.VMEM((n_gx, chunk, 4 * C), F32),
            dma((n_gy - 1,)), dma((n_gy - 1,)),
            dma((n_gx - 1,)), dma((n_gx - 1,)),
            dma((n_gy - 1,)), dma((n_gy - 1,)),
        ],
        compiler_params=pltpu.CompilerParams(collective_id=1, has_side_effects=True),
    )(grads)
    u1, u2, u3 = pl.pallas_call(
        finish_kernel,
        name="update",
        out_shape=[shape(conv_one.shape, F32), shape(conv_two.shape, F32), shape(head.shape, F32)],
        in_specs=[VM] * 5,
        out_specs=[VM] * 3,
    )(summed, d1, d2, d3, ids.reshape(1, -1))
    return final, u1, u2, u3


def solution(mesh):
    grid = P(None, "gx", "gy")
    placed = (grid, grid, P("gx", "gy")) + (P(),) * 7
    return jax.shard_map(
        functools.partial(per_device, (mesh.shape["gx"], mesh.shape["gy"])),
        mesh=mesh,
        in_specs=placed,
        out_specs=(grid, P(), P(), P()),
        check_vma=False,
    )
```
